32 devices in a mesh: groups: 2 (over x), seq: 16 (over z, y, core).
Axes of the slice: x: 2, y: 2, z: 4, core: 2. Of those that a mesh axis runs over, the one named last changes fastest.
Arguments:
- tokens: bfloat16 [8192, 4096], P(('groups', 'seq')), parts along dimension 0, may hold values from -14 to 14, as said below
- norm_gain: float32 [4096], replicated, may hold values from 0.25 to 1.75
- w_query: bfloat16 [4096, 2048], P('seq'), may hold values from -1 to 1, as said below
- w_key: bfloat16 [4096, 512], P('seq'), may hold values from -24 to 24
- w_value: bfloat16 [4096, 512], P('seq'), may hold values from -0.09375 to 0.09375
- passage_blocks: int32 [64], P(('groups', 'seq')), parts along dimension 0, may hold values from 0 to 9, as said below
Outputs:
- attended: bfloat16 [8192, 2048], P(('groups', 'seq')), parts along dimension 0
The draws below stay inside these ranges and needn't reach their ends.
There are 2 independent parts, one for each index of `groups`. The reference program is written for one: setup_inputs(seed, part) draws one part's arguments, and reference() takes and returns one part's arrays. A program takes and returns all parts, laid end to end along the dimension named above; an argument that names none is the same for every part. Nothing has to cross between parts.
Inputs may be any that keep to these rules, and one draw needn't show every extreme that they name: `passage_blocks`: passage numbers never fall along the row; each passage covers 1 to 7 whole blocks; the first and the last passage of the row cover exactly 7. `tokens`: hidden states of order one. `w_query`: entries of order 4096 ** -0.5.
All inputs are finite; a program needn't handle non-finite values.
Results may differ from the reference program's by a relative error of at most 0.0049.
The reference program's roundings to bfloat16 on the way (of `normed`, `query` and `rounded`) count: a program that leaves them out, or rounds other values in their place, can miss the bound.
Values may be sent and summed in bfloat16 or wider, within the bound.
A program may use at most 128 MiB of HBM per device.

```python
import jax
import jax.numpy as jnp
from jax import lax

D = 4096
HD = 128
QH = 16
KVH = 4
BLOCK = 128
REACH = 3
TOK_DEV = 256
NBLK = 32
TOKENS = 4096
MOST_BLK = 7
PASSAGES = 10
N_SEQ = 16


def query_matrix(key):
    sample = jax.random.normal(jax.random.fold_in(key, 11), (D, QH * HD), jnp.float32)
    return jnp.clip(sample, -6.0, 6.0) * D ** (-0.5)


def draw_w_query(key, part):
    return query_matrix(key).astype(jnp.bfloat16)


def draw_w_key(key, part):
    jitter = jnp.clip(jax.random.normal(jax.random.fold_in(key, 12), (D, KVH * HD), jnp.float32), -6.0, 6.0) * D ** (-0.5)
    return jitter.astype(jnp.bfloat16)


def draw_tokens(key, part):
    sample = jax.random.normal(jax.random.fold_in(key, 23), (TOKENS, D), jnp.float32)
    return jnp.clip(sample, -6.0, 6.0).astype(jnp.bfloat16)


def draw_passage_blocks(key, part):
    middle_blocks = NBLK - 2 * MOST_BLK
    middle_count = PASSAGES - 2
    extra_total = middle_blocks - middle_count
    slots = middle_count * (MOST_BLK - 1)
    order = jax.random.permutation(jax.random.fold_in(key, 31), slots)
    owners = (order[:extra_total] // (MOST_BLK - 1)).astype(jnp.int32)
    labels = jnp.arange(middle_count, dtype=jnp.int32)
    extra = jnp.sum((owners[:, None] == labels[None, :]).astype(jnp.int32), axis=0)
    lengths = 1 + extra
    ends = jnp.cumsum(lengths).astype(jnp.int32)
    positions = jnp.arange(middle_blocks, dtype=jnp.int32)
    middle_ids = 1 + jnp.sum((positions[:, None] >= ends[None, :]).astype(jnp.int32), axis=1)
    head_ids = jnp.zeros((MOST_BLK,), jnp.int32)
    tail_ids = jnp.full((MOST_BLK,), PASSAGES - 1, jnp.int32)
    return jnp.concatenate([head_ids, middle_ids.astype(jnp.int32), tail_ids]).astype(jnp.int32)


def level_of(stream_key, extent, cuts, low, largest):
    gain = 1.0
    for position, parts in cuts:
        draws = jax.random.uniform(jax.random.fold_in(jax.random.fold_in(stream_key, 6), position), (parts,), jnp.float32, low / len(cuts), largest / len(cuts))
        gain = gain * jnp.repeat(jnp.exp(draws), extent[position] // parts).reshape((-1,) + (1,) * (len(extent) - 1 - position))
    return gain


def scatter_about(stream_key, shape, deviation, reach, shards=(), kind=jnp.bfloat16):
    drawn = jax.random.normal(stream_key, shape, jnp.float32) * deviation
    if len(shards) > 0:
        drawn = level_of(stream_key, shape, shards, -0.22, 0.18) * drawn
    return jnp.clip(drawn, min=-reach, max=reach).astype(kind)


def setup_inputs(seed: int = 0, part: int = 0) -> dict:
    key_of = jax.random.split(jax.random.key(seed), 7)
    own_keys = jax.random.split(jax.random.fold_in(key_of[6], part), 7)
    return {
        "tokens": draw_tokens(jax.random.fold_in(jax.random.fold_in(key_of[6], part), 71), part),
        "norm_gain": jnp.clip(1.0 + 0.15 * jax.random.normal(key_of[1], (D,), jnp.float32), 0.25, 1.75),
        "w_query": draw_w_query(jax.random.fold_in(key_of[6], 71), part),
        "w_key": draw_w_key(jax.random.fold_in(key_of[6], 71), part),
        "w_value": scatter_about(key_of[4], (D, KVH * HD), D ** -0.5, 0.09375, ((0, 16),)),
        "passage_blocks": draw_passage_blocks(jax.random.fold_in(jax.random.fold_in(key_of[6], part), 71), part),
    }


def normalize(tokens, norm_gain):
    widened = tokens.astype(jnp.float32)
    inverse = lax.rsqrt(lax.optimization_barrier(jnp.mean(widened * widened, axis=-1, keepdims=True)) + 1e-05)
    return (widened * inverse * norm_gain).astype(jnp.bfloat16)

def attend_window(query, keys, values, query_ids, key_ids):
    row_count = query.shape[0]
    key_count = keys.shape[0]
    group = QH // KVH
    query_heads = query.reshape(row_count, KVH, group, HD).transpose(1, 0, 2, 3)
    key_heads = keys.reshape(key_count, KVH, HD).transpose(1, 0, 2)
    value_heads = values.reshape(key_count, KVH, HD).transpose(1, 0, 2)
    allowed = query_ids[:, None] == key_ids[None, :]

    def one_head(operands):
        head_query, head_keys, head_values = operands
        scores = jnp.einsum('tgd,sd->gts', head_query.astype(jnp.float32), head_keys.astype(jnp.float32)) * HD ** (-0.5)
        scores = jnp.where(allowed[None], scores, -1e+30)
        row_max = lax.optimization_barrier(jnp.max(scores, axis=-1, keepdims=True))
        weights = jnp.exp(scores - row_max)
        row_total = lax.optimization_barrier(jnp.sum(weights, axis=-1, keepdims=True))
        rounded = lax.optimization_barrier(weights.astype(jnp.bfloat16))
        mixed = jnp.einsum('gts,sd->tgd', rounded.astype(jnp.float32), head_values.astype(jnp.float32))
        return mixed / row_total.transpose(1, 0, 2)
    stacked = lax.map(one_head, (query_heads, key_heads, value_heads))
    return stacked.transpose(1, 0, 2, 3).reshape(row_count, QH * HD)

def reference(tokens, norm_gain, w_query, w_key, w_value, passage_blocks):
    normed = normalize(tokens, norm_gain)
    query = jnp.dot(normed, w_query, preferred_element_type=jnp.float32).astype(jnp.bfloat16)
    keys = jnp.dot(normed, w_key, preferred_element_type=jnp.float32).astype(jnp.bfloat16)
    values = jnp.dot(normed, w_value, preferred_element_type=jnp.float32).astype(jnp.bfloat16)
    passage = jnp.repeat(passage_blocks + 1, BLOCK).astype(jnp.int32)
    margin = REACH * TOK_DEV
    keys_wide = jnp.pad(keys, ((margin, margin), (0, 0)))
    values_wide = jnp.pad(values, ((margin, margin), (0, 0)))
    passage_wide = jnp.pad(passage, (margin, margin))
    window_len = (2 * REACH + 1) * TOK_DEV

    def one_shard(index):
        first_row = (index * TOK_DEV).astype(jnp.int32)
        shard_query = lax.dynamic_slice_in_dim(query, first_row, TOK_DEV, 0)
        shard_ids = lax.dynamic_slice_in_dim(passage, first_row, TOK_DEV, 0)
        near_keys = lax.dynamic_slice_in_dim(keys_wide, first_row, window_len, 0)
        near_values = lax.dynamic_slice_in_dim(values_wide, first_row, window_len, 0)
        near_ids = lax.dynamic_slice_in_dim(passage_wide, first_row, window_len, 0)
        return attend_window(shard_query, near_keys, near_values, shard_ids, near_ids).astype(jnp.bfloat16)
    result = lax.map(one_shard, jnp.arange(N_SEQ, dtype=jnp.int32))
    return result.reshape(TOKENS, QH * HD)
```

```python
import functools
import math

import jax
import jax.numpy as jnp
from jax import lax
from jax.experimental import pallas as pl
from jax.experimental.pallas import tpu as pltpu
from jax.sharding import PartitionSpec as P

HD = 128
QH = 16
KVH = 4
REACH = 3
GQ = QH // KVH
MESH = pl.DeviceIdType.MESH
SETS = 3
SW = 2 * HD
PIECES = 4
SLOTS = 2 * REACH + 2


def kernel(n_chips, tok_ref, gain_ref, wq_ref, wk_ref, wv_ref, id_ref, out_ref,
           xraw, xn, wkv, wq0, wq1, qbuf, win, idwin, obuf,
           send_sem, loc_sem, init_sem, zsem, ysem, hsem, tok_sem, id_sem, halo_sem, out_sem):
    nz = n_chips // 2
    rows, width = tok_ref.shape
    depth = wq_ref.shape[0]
    chunk = 2 * depth
    nblk = 2
    blk = rows // nblk
    g = lax.axis_index("groups")
    s = lax.axis_index("seq")
    gx = lax.rem(g, 2)
    gp = g + 1 - 2 * gx
    c = lax.rem(s, 2)
    p = s // 2
    y = lax.rem(p, 2)
    z = p // 2
    me4 = 2 * gx + c
    sib4 = 2 * gx + 1 - c
    xs4 = 2 * (1 - gx) + c
    xo4 = 2 * (1 - gx) + 1 - c
    zpair_right = lax.rem(z, 2) == 0

    def at_chip(q):
        return (g, 2 * q + c)

    sib = (g, 2 * p + 1 - c)
    xsame = (gp, s)
    xother = (gp, 2 * p + 1 - c)
    ypart = at_chip(p + 1 - 2 * y)
    zm, zp = at_chip(p - 2), at_chip(p + 2)
    has_zm, has_zp = z >= 1, z + 1 < nz
    zpair = at_chip(p + 2 - 4 * lax.rem(z, 2))

    sends = []
    counter = [0]

    def next_sem():
        counter[0] += 1
        return counter[0] - 1

    def guarded(cond, f):
        if cond is None:
            f()
        else:
            pl.when(cond)(f)

    def send(src, dst, rsem, dev, cond=None, idx=None):
        i = next_sem() if idx is None else idx
        d = pltpu.make_async_remote_copy(src_ref=src, dst_ref=dst, send_sem=send_sem.at[i],
                                         recv_sem=rsem, device_id=dev, device_id_type=MESH)
        guarded(cond, d.start)
        sends.append((cond, d))

    def recv(dst, rsem, dev, cond=None):
        d = pltpu.make_async_remote_copy(src_ref=dst, dst_ref=dst, send_sem=send_sem.at[0],
                                         recv_sem=rsem, device_id=dev, device_id_type=MESH)
        guarded(cond, d.wait_recv)

    def local(src, dst, i):
        d = pltpu.make_async_copy(src, dst, loc_sem.at[i])
        d.start()
        return d

    def cols(ref, head, width_, off=0):
        start = pl.multiple_of(head * (width_ if off is None else width_) + 0, HD)
        return ref.at[:, pl.ds(start, width_)]

    def qcols(head, half):
        return wq_ref.at[:, pl.ds(pl.multiple_of(head * (GQ * HD) + half * SW, HD), SW)]

    def own_rows(core):
        return pl.ds(pl.multiple_of(p * chunk + core * depth, depth), depth)

    bufs = (wkv, wq0, wq1)

    def parts(head, core):
        r = own_rows(core)
        return ((cols(wk_ref, head, HD), wkv.at[r, 0:HD]),
                (cols(wv_ref, head, HD), wkv.at[r, HD:SW]),
                (qcols(head, 0), wq0.at[r, :]),
                (qcols(head, 1), wq1.at[r, :]))

    loc_w = [local(a, b, i) for i, (a, b) in enumerate(parts(me4, c))]
    loc_x = local(tok_ref, xraw.at[me4], 4)
    loc_id = local(id_ref, idwin.at[gx, REACH + c], 5)

    def blank(lo, hi):
        def f():
            win[:, lo:hi] = jnp.zeros((2, hi - lo, rows, SW), jnp.bfloat16)
            idwin[:, lo:hi] = jnp.zeros((2, hi - lo) + id_ref.shape, jnp.int32)
        return f

    pl.when(p < 2)(blank(0, 1))
    pl.when(p < 1)(blank(1, 3))
    pl.when(p + 1 >= n_chips)(blank(5, 7))
    pl.when(p + 2 >= n_chips)(blank(7, 8))

    barrier = pltpu.get_barrier_semaphore()
    diag_up = (y == 1) & has_zp
    diag_dn = (y == 0) & has_zm
    for dev in (sib, xsame, xother, ypart):
        pl.semaphore_signal(barrier, inc=1, device_id=dev, device_id_type=MESH)
    for cond, dev in ((has_zm, zm), (has_zp, zp), (diag_up, at_chip(p + 1)), (diag_dn, at_chip(p - 1))):
        guarded(cond, functools.partial(pl.semaphore_signal, barrier, inc=1, device_id=dev, device_id_type=MESH))
    peers = sum(jnp.where(cond, 1, 0) for cond in (has_zm, has_zp, diag_up, diag_dn))
    pl.semaphore_wait(barrier, 4 + peers)

    for i, (a, b) in enumerate(parts(sib4, c)):
        send(a, b, init_sem.at[i], sib)
    prow = rows // PIECES
    for j in range(PIECES):
        r = slice(j * prow, (j + 1) * prow)
        send(tok_ref.at[r], xraw.at[me4, r], tok_sem.at[0, j], xsame)
    send(tok_ref, xraw.at[me4], tok_sem.at[2, 0], sib)
    for i, dev in enumerate((sib, xsame, xother)):
        send(id_ref, idwin.at[gx, REACH + c], id_sem.at[i], dev)

    def wchunk(buf, zz, yy, half=None):
        if half is None:
            return buf.at[pl.ds(pl.multiple_of((2 * zz + yy) * chunk, chunk), chunk)]
        return buf.at[pl.ds(pl.multiple_of((2 * zz + yy) * chunk + half * depth, depth), depth)]

    def relay(t, d):
        buf = bufs[t]
        if d == 0:
            for i in ((0, 1) if t == 0 else (t + 1,)):
                loc_w[i].wait()
                src, dst = parts(me4, 1 - c)[i]
                recv(dst, init_sem.at[i], sib)
            own = wchunk(buf, z, y)
            send(own, own, zsem.at[t, 1, 1], zm, has_zm)
            send(own, own, zsem.at[t, 0, 1], zp, has_zp)
            send(own, own, ysem.at[t, 0, 0], ypart)
            return
        left = wchunk(buf, z - d, y)
        right = wchunk(buf, z + d, y)
        has_l, has_r = z >= d, z + d < nz
        recv(right, zsem.at[t, 1, d], zp, has_r)
        if d + 1 < nz:
            send(right, right, zsem.at[t, 1, d + 1], zm, has_r & has_zm)
        recv(left, zsem.at[t, 0, d], zm, has_l)
        if d + 1 < nz:
            send(left, left, zsem.at[t, 0, d + 1], zp, has_l & has_zp)
        if d == 1:
            i, k = next_sem(), next_sem()
            rh, lh = wchunk(buf, z + 1, y, 0), wchunk(buf, z - 1, y, 0)
            odd = lax.rem(z, 2) == 1
            send(rh, rh, ysem.at[t, 1, 1], ypart, zpair_right, i)
            send(right, right, ysem.at[t, 1, 1], ypart, odd & has_r, i)
            send(lh, lh, ysem.at[t, 0, 1], ypart, odd, k)
            send(left, left, ysem.at[t, 0, 1], ypart, zpair_right & has_l, k)
            mate = wchunk(buf, z, 1 - y)
            recv(mate, ysem.at[t, 0, 0], ypart)
            mh = wchunk(buf, z, 1 - y, 1)
            send(mh, mh, hsem.at[t], zpair)
        else:
            send(right, right, ysem.at[t, 1, d], ypart, has_r)
            send(left, left, ysem.at[t, 0, d], ypart, has_l)

    def finish(t):
        buf = bufs[t]
        odd = lax.rem(z, 2) == 1
        for d in range(1, nz):
            right, left = wchunk(buf, z + d, 1 - y), wchunk(buf, z - d, 1 - y)
            has_l, has_r = z >= d, z + d < nz
            if d == 1:
                recv(wchunk(buf, z + 1, 1 - y, 0), ysem.at[t, 1, 1], ypart, zpair_right)
                recv(right, ysem.at[t, 1, 1], ypart, odd & has_r)
                recv(wchunk(buf, z - 1, 1 - y, 0), ysem.at[t, 0, 1], ypart, odd)
                recv(left, ysem.at[t, 0, 1], ypart, zpair_right & has_l)
            else:
                recv(right, ysem.at[t, 1, d], ypart, has_r)
                recv(left, ysem.at[t, 0, d], ypart, has_l)
        mh = wchunk(buf, z + 1 - 2 * lax.rem(z, 2), 1 - y, 1)
        recv(mh, hsem.at[t], zpair)

    def normalize(slot):
        step = 16

        def body(i, _):
            r = pl.ds(pl.multiple_of(i * step, step), step)
            wide = xraw[slot, r, :].astype(jnp.float32)
            inv = lax.rsqrt(jnp.mean(wide * wide, axis=-1, keepdims=True) + 1e-05)
            xn[slot, r, :] = (wide * inv * gain_ref[...]).astype(jnp.bfloat16)
            return 0

        lax.fori_loop(0, rows // step, body, 0)

    def forward_tokens(j):
        r = slice(j * prow, (j + 1) * prow)
        recv(xraw.at[xs4, r], tok_sem.at[0, j], xsame)
        send(xraw.at[xs4, r], xraw.at[xs4, r], tok_sem.at[1, j], sib)

    def project_kv(gi):
        def body(ci, _):
            r = jnp.dot(xn[2 * gi + ci], wkv[...], preferred_element_type=jnp.float32)
            win[gi, REACH + ci] = r.astype(jnp.bfloat16)
            return 0

        lax.fori_loop(0, 2, body, 0)

    def project_q(t):
        buf = bufs[t]

        def body(i, _):
            r = jnp.dot(xn[i], buf[...], preferred_element_type=jnp.float32).astype(jnp.bfloat16)
            qbuf[2 * (t - 1), i] = r[:, 0:HD]
            qbuf[2 * (t - 1) + 1, i] = r[:, HD:SW]
            return 0

        lax.fori_loop(0, 4, body, 0)

    up1, dn1, up2, dn2 = p + 1 < n_chips, p >= 1, p + 2 < n_chips, p >= 2
    routes = ((up1, p + 1, (3, 5), (1, 3)), (dn1, p - 1, (3, 5), (5, 7)),
              (up2, p + 2, (4, 5), (0, 1)), (dn2, p - 2, (3, 4), (7, 8)))
    back = ((dn1, p - 1), (up1, p + 1), (dn2, p - 2), (up2, p + 2))

    def halo_send(gi, which):
        for i, (cond, q, a, b) in enumerate(routes):
            send(win.at[gi, a[0]:a[1]], win.at[gi, b[0]:b[1]], halo_sem.at[which, i], at_chip(q), cond)

    def halo_recv(gi, which):
        for i, (_, _, a, b) in enumerate(routes):
            cond, q = back[i]
            recv(win.at[gi, b[0]:b[1]], halo_sem.at[which, i], at_chip(q), cond)

    def ids_send():
        loc_id.wait()
        recv(idwin.at[gx, REACH + 1 - c], id_sem.at[0], sib)
        recv(idwin.at[1 - gx, REACH + c], id_sem.at[1], xsame)
        recv(idwin.at[1 - gx, REACH + 1 - c], id_sem.at[2], xother)
        for i, (cond, q, a, b) in enumerate(routes):
            send(idwin.at[:, a[0]:a[1]], idwin.at[:, b[0]:b[1]], id_sem.at[3 + i], at_chip(q), cond)

    def ids_recv():
        for i, (_, _, a, b) in enumerate(routes):
            cond, q = back[i]
            recv(idwin.at[:, b[0]:b[1]], id_sem.at[3 + i], at_chip(q), cond)

    rate = HD ** (-0.5) * math.log2(math.e)
    span = 2 * REACH + 1

    def attend(gi, ci, t):
        slot = 2 * gi + ci
        key_ids = jnp.concatenate([idwin[gi, ci + j, 0:1, :] for j in range(span)], axis=1)
        for qb in range(nblk):
            mine = idwin[gi, REACH + ci, 0:1, qb * blk:qb * blk + HD]
            allowed = key_ids == jnp.concatenate([mine] * (span * rows // HD), axis=1)
            rr = slice(qb * blk, (qb + 1) * blk)

            def head(hh, _):
                q = qbuf[2 * t + hh, slot, rr, :]
                k = win[gi, pl.ds(ci, span), :, 0:HD].reshape(span * rows, HD)
                v = win[gi, pl.ds(ci, span), :, HD:SW].reshape(span * rows, HD)
                sc = lax.dot_general(q, k, (((1,), (1,)), ((), ())), preferred_element_type=jnp.float32)
                sc = jnp.where(allowed, sc, -1e30)
                top = jnp.max(sc, axis=-1, keepdims=True)
                w = jnp.exp2((sc - top) * rate)
                total = jnp.sum(w, axis=-1, keepdims=True)
                mixed = jnp.dot(w.astype(jnp.bfloat16), v, preferred_element_type=jnp.float32)
                obuf[t, slot, rr, pl.ds(pl.multiple_of(hh * HD, HD), HD)] = (mixed / total).astype(jnp.bfloat16)
                return 0

            lax.fori_loop(0, 2, head, 0)

    def out_cols(head, t):
        return out_ref.at[:, pl.ds(pl.multiple_of(head * (GQ * HD) + t * SW, HD), SW)]

    out_local = []

    def attend_set(t):
        for i, (gi, ci, dev) in enumerate(((1 - gx, 1 - c, xother), (1 - gx, c, xsame), (gx, 1 - c, sib), (gx, c, None))):
            attend(gi, ci, t)
            src = obuf.at[t, 2 * gi + ci]
            if dev is None:
                out_local.append(local(src, out_cols(me4, t), 6 + t))
            else:
                send(src, out_cols(me4, t), out_sem.at[t, i], dev)

    relay(0, 0)
    loc_x.wait()
    normalize(me4)
    relay(1, 0)
    relay(0, 1)
    ids_send()
    recv(xraw.at[sib4], tok_sem.at[2, 0], sib)
    normalize(sib4)
    last = nz - 1 + SETS - 1
    for w in range(2, last + 1):
        for t in range(SETS):
            d = w - t
            if 0 <= d < nz:
                relay(t, d)
        if w == 2:
            forward_tokens(0)
        if w == 3:
            forward_tokens(1)
            forward_tokens(2)
        if w == last - 1:
            finish(0)
            project_kv(gx)
            halo_send(gx, 0)
    forward_tokens(3)
    for j in range(PIECES):
        r = slice(j * prow, (j + 1) * prow)
        recv(xraw.at[xo4, r], tok_sem.at[1, j], sib)
    normalize(xs4)
    normalize(xo4)
    project_kv(1 - gx)
    halo_send(1 - gx, 1)
    finish(1)
    project_q(1)
    ids_recv()
    halo_recv(gx, 0)
    halo_recv(1 - gx, 1)
    attend_set(0)
    finish(2)
    project_q(2)
    attend_set(1)
    for t in range(2):
        for i, (dev, head) in enumerate(((xother, xo4), (xsame, xs4), (sib, sib4))):
            recv(out_cols(head, t), out_sem.at[t, i], dev)
    for d in out_local:
        d.wait()
    for cond, d in sends:
        guarded(cond, d.wait_send)


def solution(mesh):
    n_seq = mesh.shape["seq"]
    n_chips = n_seq // 2
    nz = n_chips // 2

    def on_device(tokens, norm_gain, w_query, w_key, w_value, passage_blocks):
        rows, width = tokens.shape
        ids = jnp.repeat(passage_blocks + 1, rows // passage_blocks.shape[0])
        ids = jnp.broadcast_to(ids[None, :], (8, rows))
        anywhere = pl.BlockSpec(memory_space=pl.ANY)
        vmem = pl.BlockSpec(memory_space=pltpu.VMEM)
        n_send = SETS * (4 * nz) + 4 + 2 * PIECES + 1 + 3 + 8 + 4 + 6 + 8
        bf = jnp.bfloat16
        dma = pltpu.SemaphoreType.DMA
        return pl.pallas_call(
            functools.partial(kernel, n_chips),
            out_shape=jax.ShapeDtypeStruct((rows, QH * HD), bf),
            in_specs=[anywhere, vmem, anywhere, anywhere, anywhere, anywhere],
            out_specs=anywhere,
            scratch_shapes=[
                pltpu.VMEM((4, rows, width), bf),
                pltpu.VMEM((4, rows, width), bf),
                pltpu.VMEM((width, SW), bf),
                pltpu.VMEM((width, SW), bf),
                pltpu.VMEM((width, SW), bf),
                pltpu.VMEM((GQ, 4, rows, HD), bf),
                pltpu.VMEM((2, SLOTS, rows, SW), bf),
                pltpu.VMEM((2, SLOTS, 8, rows), jnp.int32),
                pltpu.VMEM((2, 4, rows, SW), bf),
                dma((n_send,)), dma((8,)), dma((4,)), dma((SETS, 2, nz)), dma((SETS, 2, nz)),
                dma((SETS,)), dma((3, PIECES)), dma((7,)), dma((2, 4)), dma((2, 3)),
            ],
            compiler_params=pltpu.CompilerParams(
                collective_id=0, has_side_effects=True, vmem_limit_bytes=60 * 2**20),
        )(tokens, norm_gain[None, :], w_query, w_key, w_value, ids)

    in_specs = (
        P(("groups", "seq"), None),
        P(),
        P("seq", None),
        P("seq", None),
        P("seq", None),
        P(("groups", "seq")),
    )
    out_specs = P(("groups", "seq"), None)
    return jax.shard_map(on_device, mesh=mesh, in_specs=in_specs, out_specs=out_specs, check_vma=False)
```

```python
import functools
import math

import jax
import jax.numpy as jnp
from jax import lax
from jax.experimental import pallas as pl
from jax.experimental.pallas import tpu as pltpu
from jax.sharding import PartitionSpec as P

HD = 128
QH = 16
KVH = 4
REACH = 3
GQ = QH // KVH
MESH = pl.DeviceIdType.MESH
SETS = 3
SW = 2 * HD
PIECES = 4
SLOTS = 2 * REACH + 4


def kernel(n_chips, tok_ref, gain_ref, wq_ref, wk_ref, wv_ref, id_ref, out_ref,
           xraw, xn, wkv, wq0, wq1, qbuf, win, idwin, obuf,
           send_sem, loc_sem, init_sem, zsem, xsem, tok_sem, id_sem, halo_sem, out_sem):
    nz = n_chips // 2
    rows, width = tok_ref.shape
    nblk = 2
    blk = rows // nblk
    g = lax.axis_index("groups")
    s = lax.axis_index("seq")
    gx = lax.rem(g, 2)
    gp = g + 1 - 2 * gx
    c = lax.rem(s, 2)
    p = s // 2
    y = lax.rem(p, 2)
    z = p // 2
    me4 = 2 * y + c
    sib4 = 2 * y + 1 - c
    ys4 = 2 * (1 - y) + c
    yo4 = 2 * (1 - y) + 1 - c

    sib = (g, 4 * z + sib4)
    ysame = (g, 4 * z + ys4)
    yother = (g, 4 * z + yo4)
    twin = (gp, s)
    zm, zp = (g, s - 4), (g, s + 4)
    has_zm, has_zp = z >= 1, z + 1 < nz

    sends = []
    counter = [0]

    def guarded(cond, f):
        if cond is None:
            f()
        else:
            pl.when(cond)(f)

    def send(src, dst, rsem, dev, cond=None):
        d = pltpu.make_async_remote_copy(src_ref=src, dst_ref=dst, send_sem=send_sem.at[counter[0]],
                                         recv_sem=rsem, device_id=dev, device_id_type=MESH)
        counter[0] += 1
        guarded(cond, d.start)
        sends.append((cond, d))

    def recv(dst, rsem, dev, cond=None):
        d = pltpu.make_async_remote_copy(src_ref=dst, dst_ref=dst, send_sem=send_sem.at[0],
                                         recv_sem=rsem, device_id=dev, device_id_type=MESH)
        guarded(cond, d.wait_recv)

    def local(src, dst, i):
        d = pltpu.make_async_copy(src, dst, loc_sem.at[i])
        d.start()
        return d

    bufs = (wkv, wq0, wq1)

    def columns(head, i):
        if i < 2:
            return pl.ds(pl.multiple_of(head * HD, HD), HD)
        return pl.ds(pl.multiple_of(head * (GQ * HD) + (i - 2) * SW, HD), SW)

    weights = (wk_ref, wv_ref, wq_ref, wq_ref)
    places = ((wkv, slice(0, HD)), (wkv, slice(HD, SW)), (wq0, slice(0, SW)), (wq1, slice(0, SW)))

    def full_part(i, head, yy, cc):
        buf, lanes = places[i]
        return weights[i].at[:, :, columns(head, i)], buf.at[z, yy, cc, :, :, lanes]

    def half_part(i, head, yy, cc):
        buf, lanes = places[i]
        return weights[i].at[gx, :, columns(head, i)], buf.at[z, yy, cc, gx, :, lanes]

    loc_w = [local(*full_part(i, me4, y, c), i) for i in range(4)]
    loc_x = local(tok_ref, xraw.at[me4], 4)
    loc_id = local(id_ref, idwin.at[REACH + me4], 5)

    def blank(lo):
        def f():
            win[lo:lo + REACH] = jnp.zeros((REACH, rows, SW), jnp.bfloat16)
            idwin[lo:lo + REACH] = jnp.zeros((REACH,) + id_ref.shape, jnp.int32)
        return f

    pl.when(z < 1)(blank(0))
    pl.when(z + 1 >= nz)(blank(REACH + 4))

    barrier = pltpu.get_barrier_semaphore()
    for dev in (sib, ysame, yother, twin):
        pl.semaphore_signal(barrier, inc=1, device_id=dev, device_id_type=MESH)
    for cond, dev in ((has_zm, zm), (has_zp, zp)):
        guarded(cond, functools.partial(pl.semaphore_signal, barrier, inc=1, device_id=dev, device_id_type=MESH))
    pl.semaphore_wait(barrier, 4 + jnp.where(has_zm, 1, 0) + jnp.where(has_zp, 1, 0))

    prow = rows // PIECES
    for i in range(4):
        for k, (dev, head) in enumerate(((ysame, ys4), (yother, yo4))):
            a, b = half_part(i, head, y, c)
            send(a, b, init_sem.at[i, 1 + k], dev)
        a, b = full_part(i, sib4, y, c)
        send(a, b, init_sem.at[i, 0], sib)
    for i, dev in enumerate((sib, ysame, yother)):
        send(id_ref, idwin.at[REACH + me4], id_sem.at[i], dev)
    for j in range(PIECES):
        r = slice(j * prow, (j + 1) * prow)
        send(tok_ref.at[r], xraw.at[me4, r], tok_sem.at[0, j], ysame)
    send(tok_ref, xraw.at[me4], tok_sem.at[2, 0], sib)

    def relay(t, d):
        buf = bufs[t]
        if d == 0:
            for i in ((0, 1) if t == 0 else (t + 1,)):
                loc_w[i].wait()
                recv(full_part(i, me4, y, 1 - c)[1], init_sem.at[i, 0], sib)
                recv(half_part(i, me4, 1 - y, c)[1], init_sem.at[i, 1], ysame)
                recv(half_part(i, me4, 1 - y, 1 - c)[1], init_sem.at[i, 2], yother)
            own = buf.at[z, :, :, gx]
            send(own, own, zsem.at[t, 1, 1], zm, has_zm)
            send(own, own, zsem.at[t, 0, 1], zp, has_zp)
            mate = buf.at[z, 1 - y, :, gx]
            send(mate, mate, xsem.at[t, 0, 0], twin)
            return
        left = buf.at[z - d, :, :, gx]
        right = buf.at[z + d, :, :, gx]
        has_l, has_r = z >= d, z + d < nz
        recv(right, zsem.at[t, 1, d], zp, has_r)
        if d + 1 < nz:
            send(right, right, zsem.at[t, 1, d + 1], zm, has_r & has_zm)
        recv(left, zsem.at[t, 0, d], zm, has_l)
        if d + 1 < nz:
            send(left, left, zsem.at[t, 0, d + 1], zp, has_l & has_zp)
        send(right, right, xsem.at[t, 1, d], twin, has_r)
        send(left, left, xsem.at[t, 0, d], twin, has_l)

    def finish(t):
        buf = bufs[t]
        recv(buf.at[z, 1 - y, :, 1 - gx], xsem.at[t, 0, 0], twin)
        for d in range(1, nz):
            recv(buf.at[z + d, :, :, 1 - gx], xsem.at[t, 1, d], twin, z + d < nz)
            recv(buf.at[z - d, :, :, 1 - gx], xsem.at[t, 0, d], twin, z >= d)

    def normalize(slot):
        step = 16

        def body(i, _):
            r = pl.ds(pl.multiple_of(i * step, step), step)
            wide = xraw[slot, r, :].astype(jnp.float32)
            inv = lax.rsqrt(jnp.mean(wide * wide, axis=-1, keepdims=True) + 1e-05)
            xn[slot, r, :] = (wide * inv * gain_ref[...]).astype(jnp.bfloat16)
            return 0

        lax.fori_loop(0, rows // step, body, 0)

    def forward_tokens(j):
        r = slice(j * prow, (j + 1) * prow)
        recv(xraw.at[ys4, r], tok_sem.at[0, j], ysame)
        send(xraw.at[ys4, r], xraw.at[ys4, r], tok_sem.at[1, j], sib)

    def project_kv(yy):
        def body(ci, _):
            r = jnp.dot(xn[2 * yy + ci], wkv[...].reshape(width, SW), preferred_element_type=jnp.float32)
            win[REACH + 2 * yy + ci] = r.astype(jnp.bfloat16)
            return 0

        lax.fori_loop(0, 2, body, 0)

    def project_q(t):
        buf = bufs[t]

        def body(i, _):
            r = jnp.dot(xn[i], buf[...].reshape(width, SW), preferred_element_type=jnp.float32).astype(jnp.bfloat16)
            qbuf[2 * (t - 1), i] = r[:, 0:HD]
            qbuf[2 * (t - 1) + 1, i] = r[:, HD:SW]
            return 0

        lax.fori_loop(0, 4, body, 0)

    def halo_send(yy, which):
        for slot in range(4):
            mine = (slot // 2) == yy
            a = win.at[REACH + slot]
            if slot > 0:
                send(a, win.at[slot - 1], halo_sem.at[0, slot - 1], zp, mine & has_zp)
            if slot < 3:
                send(a, win.at[REACH + 4 + slot], halo_sem.at[1, slot], zm, mine & has_zm)

    def halo_recv():
        for j in range(REACH):
            recv(win.at[j], halo_sem.at[0, j], zm, has_zm)
            recv(win.at[REACH + 4 + j], halo_sem.at[1, j], zp, has_zp)

    def ids_send():
        loc_id.wait()
        for i, (slot, dev) in enumerate(((sib4, sib), (ys4, ysame), (yo4, yother))):
            recv(idwin.at[REACH + slot], id_sem.at[i], dev)
        send(idwin.at[4:7], idwin.at[0:3], id_sem.at[3], zp, has_zp)
        send(idwin.at[3:6], idwin.at[7:10], id_sem.at[4], zm, has_zm)

    def ids_recv():
        recv(idwin.at[0:3], id_sem.at[3], zm, has_zm)
        recv(idwin.at[7:10], id_sem.at[4], zp, has_zp)

    rate = HD ** (-0.5) * math.log2(math.e)
    span = 2 * REACH + 1

    def attend(slot, t):
        key_ids = jnp.concatenate([idwin[slot + j, 0:1, :] for j in range(span)], axis=1)
        for qb in range(nblk):
            mine = idwin[REACH + slot, 0:1, qb * blk:qb * blk + HD]
            allowed = key_ids == jnp.concatenate([mine] * (span * rows // HD), axis=1)
            rr = slice(qb * blk, (qb + 1) * blk)

            def head(hh, _):
                q = qbuf[2 * t + hh, slot, rr, :]
                k = win[pl.ds(slot, span), :, 0:HD].reshape(span * rows, HD)
                v = win[pl.ds(slot, span), :, HD:SW].reshape(span * rows, HD)
                sc = lax.dot_general(q, k, (((1,), (1,)), ((), ())), preferred_element_type=jnp.float32)
                sc = jnp.where(allowed, sc, -1e30)
                top = jnp.max(sc, axis=-1, keepdims=True)
                w = jnp.exp2((sc - top) * rate)
                total = jnp.sum(w, axis=-1, keepdims=True)
                mixed = jnp.dot(w.astype(jnp.bfloat16), v, preferred_element_type=jnp.float32)
                obuf[t, slot, rr, pl.ds(pl.multiple_of(hh * HD, HD), HD)] = (mixed / total).astype(jnp.bfloat16)
                return 0

            lax.fori_loop(0, 2, head, 0)

    def out_cols(head, t):
        return out_ref.at[:, pl.ds(pl.multiple_of(head * (GQ * HD) + t * SW, HD), SW)]

    out_local = []

    def attend_set(t):
        for i, (slot, dev) in enumerate(((yo4, yother), (ys4, ysame), (sib4, sib), (me4, None))):
            attend(slot, t)
            src = obuf.at[t, slot]
            if dev is None:
                out_local.append(local(src, out_cols(me4, t), 6 + t))
            else:
                send(src, out_cols(me4, t), out_sem.at[t, i], dev)

    relay(0, 0)
    loc_x.wait()
    normalize(me4)
    relay(1, 0)
    relay(0, 1)
    ids_send()
    recv(xraw.at[sib4], tok_sem.at[2, 0], sib)
    normalize(sib4)
    last = nz - 1 + SETS - 1
    for w in range(2, last + 1):
        for t in range(SETS):
            d = w - t
            if 0 <= d < nz:
                relay(t, d)
        if w == last - 2:
            forward_tokens(0)
        if w == last - 1:
            forward_tokens(1)
            finish(0)
            project_kv(y)
            halo_send(y, 0)
    for j in range(2, PIECES):
        forward_tokens(j)
    for j in range(PIECES):
        r = slice(j * prow, (j + 1) * prow)
        recv(xraw.at[yo4, r], tok_sem.at[1, j], sib)
    normalize(ys4)
    normalize(yo4)
    project_kv(1 - y)
    halo_send(1 - y, 1)
    finish(1)
    project_q(1)
    ids_recv()
    halo_recv()
    attend_set(0)
    finish(2)
    project_q(2)
    attend_set(1)
    for t in range(2):
        for i, (dev, head) in enumerate(((yother, yo4), (ysame, ys4), (sib, sib4))):
            recv(out_cols(head, t), out_sem.at[t, i], dev)
    for d in out_local:
        d.wait()
    for cond, d in sends:
        guarded(cond, d.wait_send)


def solution(mesh):
    n_seq = mesh.shape["seq"]
    n_chips = n_seq // 2
    nz = n_chips // 2

    def on_device(tokens, norm_gain, w_query, w_key, w_value, passage_blocks):
        rows, width = tokens.shape
        ids = jnp.repeat(passage_blocks + 1, rows // passage_blocks.shape[0])
        ids = jnp.broadcast_to(ids[None, :], (8, rows))
        anywhere = pl.BlockSpec(memory_space=pl.ANY)
        vmem = pl.BlockSpec(memory_space=pltpu.VMEM)
        n_send = SETS * (4 * nz) + 12 + 3 + 2 * PIECES + 1 + 2 + 12 + 6 + 2
        bf = jnp.bfloat16
        dma = pltpu.SemaphoreType.DMA
        half = w_query.shape[0] // 2
        weight = pltpu.VMEM((nz, 2, 2, 2, half, SW), bf)
        halves = [w.reshape(2, half, w.shape[1]) for w in (w_query, w_key, w_value)]
        return pl.pallas_call(
            functools.partial(kernel, n_chips),
            out_shape=jax.ShapeDtypeStruct((rows, QH * HD), bf),
            in_specs=[anywhere, vmem, anywhere, anywhere, anywhere, anywhere],
            out_specs=anywhere,
            scratch_shapes=[
                pltpu.VMEM((4, rows, width), bf),
                pltpu.VMEM((4, rows, width), bf),
                weight, weight, weight,
                pltpu.VMEM((GQ, 4, rows, HD), bf),
                pltpu.VMEM((SLOTS, rows, SW), bf),
                pltpu.VMEM((SLOTS, 8, rows), jnp.int32),
                pltpu.VMEM((2, 4, rows, SW), bf),
                dma((n_send,)), dma((8,)), dma((4, 3)), dma((SETS, 2, nz)), dma((SETS, 2, nz)),
                dma((3, PIECES)), dma((5,)), dma((2, REACH)), dma((2, 3)),
            ],
            compiler_params=pltpu.CompilerParams(
                collective_id=0, has_side_effects=True, vmem_limit_bytes=60 * 2**20),
        )(tokens, norm_gain[None, :], *halves, ids)

    in_specs = (
        P(("groups", "seq"), None),
        P(),
        P("seq", None),
        P("seq", None),
        P("seq", None),
        P(("groups", "seq")),
    )
    out_specs = P(("groups", "seq"), None)
    return jax.shard_map(on_device, mesh=mesh, in_specs=in_specs, out_specs=out_specs, check_vma=False)
```

```python
import functools
import math

import jax
import jax.numpy as jnp
from jax import lax
from jax.experimental import pallas as pl
from jax.experimental.pallas import tpu as pltpu
from jax.sharding import PartitionSpec as P

HD = 128
QH = 16
KVH = 4
REACH = 3
GQ = QH // KVH
MESH = pl.DeviceIdType.MESH
SETS = 2 + GQ
SW = 2 * HD
PIECES = 4
SLOTS = 2 * REACH + 4


def kernel(n_chips, tok_ref, gain_ref, wq_ref, wk_ref, wv_ref, id_ref, out_ref,
           xraw, xn, wkv, wq0, wq1, qbuf, win, idwin, obuf,
           send_sem, loc_sem, init_sem, zsem, xsem, tok_sem, id_sem, halo_sem, out_sem):
    nz = n_chips // 2
    rows, width = tok_ref.shape
    nblk = 2
    blk = rows // nblk
    g = lax.axis_index("groups")
    s = lax.axis_index("seq")
    gx = lax.rem(g, 2)
    gp = g + 1 - 2 * gx
    c = lax.rem(s, 2)
    p = s // 2
    y = lax.rem(p, 2)
    z = p // 2
    me4 = 2 * y + c
    sib4 = 2 * y + 1 - c
    ys4 = 2 * (1 - y) + c
    yo4 = 2 * (1 - y) + 1 - c

    sib = (g, 4 * z + sib4)
    ysame = (g, 4 * z + ys4)
    yother = (g, 4 * z + yo4)
    twin = (gp, s)
    zm, zp = (g, s - 4), (g, s + 4)
    has_zm, has_zp = z >= 1, z + 1 < nz

    sends = []
    counter = [0]

    def guarded(cond, f):
        if cond is None:
            f()
        else:
            pl.when(cond)(f)

    def send(src, dst, rsem, dev, cond=None):
        d = pltpu.make_async_remote_copy(src_ref=src, dst_ref=dst, send_sem=send_sem.at[counter[0]],
                                         recv_sem=rsem, device_id=dev, device_id_type=MESH)
        counter[0] += 1
        guarded(cond, d.start)
        sends.append((cond, d))

    def recv(dst, rsem, dev, cond=None):
        d = pltpu.make_async_remote_copy(src_ref=dst, dst_ref=dst, send_sem=send_sem.at[0],
                                         recv_sem=rsem, device_id=dev, device_id_type=MESH)
        guarded(cond, d.wait_recv)

    def local(src, dst, i):
        d = pltpu.make_async_copy(src, dst, loc_sem.at[i])
        d.start()
        return d

    bufs = (wkv, wq0, wq1)

    def columns(head, i):
        return pl.ds(pl.multiple_of(head * HD if i < 2 else head * (GQ * HD) + (i - 2) * HD, HD), HD)

    weights = (wk_ref, wv_ref) + (wq_ref,) * GQ
    places = tuple((bufs[i // 2], slice(i % 2 * HD, i % 2 * HD + HD)) for i in range(SETS))

    def unit(t, zz, half):
        buf, lanes = places[t]
        return buf.at[zz, :, :, half, :, lanes]

    def mates(t, half):
        buf, lanes = places[t]
        return buf.at[z, 1 - y, :, half, :, lanes]

    def full_part(i, head, yy, cc):
        buf, lanes = places[i]
        return weights[i].at[:, :, columns(head, i)], buf.at[z, yy, cc, :, :, lanes]

    def half_part(i, head, yy, cc):
        buf, lanes = places[i]
        return weights[i].at[gx, :, columns(head, i)], buf.at[z, yy, cc, gx, :, lanes]

    loc_w = [local(*full_part(i, me4, y, c), i) for i in range(SETS)]
    loc_x = local(tok_ref, xraw.at[me4], SETS)
    loc_id = local(id_ref, idwin.at[REACH + me4], SETS + 1)

    def blank(lo):
        def f():
            win[lo:lo + REACH] = jnp.zeros((REACH, rows, SW), jnp.bfloat16)
            idwin[lo:lo + REACH] = jnp.zeros((REACH,) + id_ref.shape, jnp.int32)
        return f

    pl.when(z < 1)(blank(0))
    pl.when(z + 1 >= nz)(blank(REACH + 4))

    barrier = pltpu.get_barrier_semaphore()
    for dev in (sib, ysame, yother, twin):
        pl.semaphore_signal(barrier, inc=1, device_id=dev, device_id_type=MESH)
    for cond, dev in ((has_zm, zm), (has_zp, zp)):
        guarded(cond, functools.partial(pl.semaphore_signal, barrier, inc=1, device_id=dev, device_id_type=MESH))
    pl.semaphore_wait(barrier, 4 + jnp.where(has_zm, 1, 0) + jnp.where(has_zp, 1, 0))

    prow = rows // PIECES
    for i in range(SETS):
        for k, (dev, head) in enumerate(((ysame, ys4), (yother, yo4))):
            a, b = half_part(i, head, y, c)
            send(a, b, init_sem.at[i, 1 + k], dev)
        a, b = full_part(i, sib4, y, c)
        send(a, b, init_sem.at[i, 0], sib)
    for i, dev in enumerate((sib, ysame, yother)):
        send(id_ref, idwin.at[REACH + me4], id_sem.at[i], dev)
    for j in range(PIECES):
        r = slice(j * prow, (j + 1) * prow)
        send(tok_ref.at[r], xraw.at[me4, r], tok_sem.at[0, j], ysame)
    send(tok_ref, xraw.at[me4], tok_sem.at[2, 0], sib)

    def relay(t, d):
        if d == 0:
            loc_w[t].wait()
            recv(full_part(t, me4, y, 1 - c)[1], init_sem.at[t, 0], sib)
            recv(half_part(t, me4, 1 - y, c)[1], init_sem.at[t, 1], ysame)
            recv(half_part(t, me4, 1 - y, 1 - c)[1], init_sem.at[t, 2], yother)
            own = unit(t, z, gx)
            send(own, own, zsem.at[t, 1, 1], zm, has_zm)
            send(own, own, zsem.at[t, 0, 1], zp, has_zp)
            send(mates(t, gx), mates(t, gx), xsem.at[t, 0, 0], twin)
            return
        left, right = unit(t, z - d, gx), unit(t, z + d, gx)
        has_l, has_r = z >= d, z + d < nz
        recv(right, zsem.at[t, 1, d], zp, has_r)
        if d + 1 < nz:
            send(right, right, zsem.at[t, 1, d + 1], zm, has_r & has_zm)
        recv(left, zsem.at[t, 0, d], zm, has_l)
        if d + 1 < nz:
            send(left, left, zsem.at[t, 0, d + 1], zp, has_l & has_zp)
        send(right, right, xsem.at[t, 1, d], twin, has_r)
        send(left, left, xsem.at[t, 0, d], twin, has_l)

    def finish(pair):
        for t in (2 * pair, 2 * pair + 1):
            recv(mates(t, 1 - gx), xsem.at[t, 0, 0], twin)
            for d in range(1, nz):
                recv(unit(t, z + d, 1 - gx), xsem.at[t, 1, d], twin, z + d < nz)
                recv(unit(t, z - d, 1 - gx), xsem.at[t, 0, d], twin, z >= d)

    def normalize(slot, first=0, count=None):
        step = 16
        count = rows if count is None else count

        def body(i, _):
            r = pl.ds(pl.multiple_of(first + i * step, step), step)
            wide = xraw[slot, r, :].astype(jnp.float32)
            inv = lax.rsqrt(jnp.mean(wide * wide, axis=-1, keepdims=True) + 1e-05)
            xn[slot, r, :] = (wide * inv * gain_ref[...]).astype(jnp.bfloat16)
            return 0

        lax.fori_loop(0, count // step, body, 0)

    def forward_tokens(j):
        r = slice(j * prow, (j + 1) * prow)
        recv(xraw.at[ys4, r], tok_sem.at[0, j], ysame)
        send(xraw.at[ys4, r], xraw.at[ys4, r], tok_sem.at[1, j], sib)
        normalize(ys4, j * prow, prow)

    def other_tokens(j):
        recv(xraw.at[yo4, j * prow:(j + 1) * prow], tok_sem.at[1, j], sib)
        normalize(yo4, j * prow, prow)

    def project_kv(yy):
        def body(ci, _):
            r = jnp.dot(xn[2 * yy + ci], wkv[...].reshape(width, SW), preferred_element_type=jnp.float32)
            win[REACH + 2 * yy + ci] = r.astype(jnp.bfloat16)
            return 0

        lax.fori_loop(0, 2, body, 0)

    def project_q(t, yy):
        buf = bufs[t]

        def body(i, _):
            i = 2 * yy + i
            r = jnp.dot(xn[i], buf[...].reshape(width, SW), preferred_element_type=jnp.float32).astype(jnp.bfloat16)
            qbuf[2 * (t - 1), i] = r[:, 0:HD]
            qbuf[2 * (t - 1) + 1, i] = r[:, HD:SW]
            return 0

        lax.fori_loop(0, 2, body, 0)

    def halo_send(yy, which):
        for slot in range(4):
            mine = (slot // 2) == yy
            a = win.at[REACH + slot]
            if slot > 0:
                send(a, win.at[slot - 1], halo_sem.at[0, slot - 1], zp, mine & has_zp)
            if slot < 3:
                send(a, win.at[REACH + 4 + slot], halo_sem.at[1, slot], zm, mine & has_zm)

    def halo_recv():
        for j in range(REACH):
            recv(win.at[j], halo_sem.at[0, j], zm, has_zm)
            recv(win.at[REACH + 4 + j], halo_sem.at[1, j], zp, has_zp)

    def ids_send():
        loc_id.wait()
        for i, (slot, dev) in enumerate(((sib4, sib), (ys4, ysame), (yo4, yother))):
            recv(idwin.at[REACH + slot], id_sem.at[i], dev)
        send(idwin.at[4:7], idwin.at[0:3], id_sem.at[3], zp, has_zp)
        send(idwin.at[3:6], idwin.at[7:10], id_sem.at[4], zm, has_zm)

    def ids_recv():
        recv(idwin.at[0:3], id_sem.at[3], zm, has_zm)
        recv(idwin.at[7:10], id_sem.at[4], zp, has_zp)

    rate = HD ** (-0.5) * math.log2(math.e)
    span = 2 * REACH + 1

    def attend(slot, t):
        key_ids = jnp.concatenate([idwin[slot + j, 0:1, :] for j in range(span)], axis=1)
        for qb in range(nblk):
            mine = idwin[REACH + slot, 0:1, qb * blk:qb * blk + HD]
            allowed = key_ids == jnp.concatenate([mine] * (span * rows // HD), axis=1)
            rr = slice(qb * blk, (qb + 1) * blk)

            def head(hh, _):
                q = qbuf[2 * t + hh, slot, rr, :]
                k = win[pl.ds(slot, span), :, 0:HD].reshape(span * rows, HD)
                v = win[pl.ds(slot, span), :, HD:SW].reshape(span * rows, HD)
                sc = lax.dot_general(q, k, (((1,), (1,)), ((), ())), preferred_element_type=jnp.float32)
                sc = jnp.where(allowed, sc, -1e30)
                top = jnp.max(sc, axis=-1, keepdims=True)
                w = jnp.exp2((sc - top) * rate)
                total = jnp.sum(w, axis=-1, keepdims=True)
                mixed = jnp.dot(w.astype(jnp.bfloat16), v, preferred_element_type=jnp.float32)
                obuf[t, slot, rr, pl.ds(pl.multiple_of(hh * HD, HD), HD)] = (mixed / total).astype(jnp.bfloat16)
                return 0

            lax.fori_loop(0, 2, head, 0)

    def out_cols(head, t):
        return out_ref.at[:, pl.ds(pl.multiple_of(head * (GQ * HD) + t * SW, HD), SW)]

    out_local = []

    def attend_set(t):
        for i, (slot, dev) in enumerate(((yo4, yother), (ys4, ysame), (sib4, sib), (me4, None))):
            attend(slot, t)
            src = obuf.at[t, slot]
            if dev is None:
                out_local.append(local(src, out_cols(me4, t), SETS + 2 + t))
            else:
                send(src, out_cols(me4, t), out_sem.at[t, i], dev)

    for t in range(SETS):
        relay(t, 0)
        if t == 2:
            loc_x.wait()
            normalize(me4)
    ids_send()
    for d in range(1, nz):
        for t in range(SETS):
            relay(t, d)
        if d == 1:
            recv(xraw.at[sib4], tok_sem.at[2, 0], sib)
            normalize(sib4)
            forward_tokens(0)
        if d == max(2, nz - 2):
            forward_tokens(1)
            other_tokens(0)
    finish(0)
    project_kv(y)
    halo_send(y, 0)
    forward_tokens(2)
    other_tokens(1)
    other_tokens(2)
    forward_tokens(3)
    other_tokens(3)
    project_kv(1 - y)
    halo_send(1 - y, 1)
    finish(1)
    project_q(1, y)
    project_q(1, 1 - y)
    ids_recv()
    halo_recv()
    attend_set(0)
    finish(2)
    project_q(2, y)
    project_q(2, 1 - y)
    attend_set(1)
    for t in range(2):
        for i, (dev, head) in enumerate(((yother, yo4), (ysame, ys4), (sib, sib4))):
            recv(out_cols(head, t), out_sem.at[t, i], dev)
    for d in out_local:
        d.wait()
    for cond, d in sends:
        guarded(cond, d.wait_send)


def solution(mesh):
    n_seq = mesh.shape["seq"]
    n_chips = n_seq // 2
    nz = n_chips // 2

    def on_device(tokens, norm_gain, w_query, w_key, w_value, passage_blocks):
        rows, width = tokens.shape
        ids = jnp.repeat(passage_blocks + 1, rows // passage_blocks.shape[0])
        ids = jnp.broadcast_to(ids[None, :], (8, rows))
        anywhere = pl.BlockSpec(memory_space=pl.ANY)
        vmem = pl.BlockSpec(memory_space=pltpu.VMEM)
        n_send = SETS * (4 * nz) + 3 * SETS + 3 + 2 * PIECES + 1 + 2 + 12 + 6 + 2
        bf = jnp.bfloat16
        dma = pltpu.SemaphoreType.DMA
        half = w_query.shape[0] // 2
        weight = pltpu.VMEM((nz, 2, 2, 2, half, SW), bf)
        halves = [w.reshape(2, half, w.shape[1]) for w in (w_query, w_key, w_value)]
        return pl.pallas_call(
            functools.partial(kernel, n_chips),
            out_shape=jax.ShapeDtypeStruct((rows, QH * HD), bf),
            in_specs=[anywhere, vmem, anywhere, anywhere, anywhere, anywhere],
            out_specs=anywhere,
            scratch_shapes=[
                pltpu.VMEM((4, rows, width), bf),
                pltpu.VMEM((4, rows, width), bf),
                weight, weight, weight,
                pltpu.VMEM((GQ, 4, rows, HD), bf),
                pltpu.VMEM((SLOTS, rows, SW), bf),
                pltpu.VMEM((SLOTS, 8, rows), jnp.int32),
                pltpu.VMEM((2, 4, rows, SW), bf),
                dma((n_send,)), dma((SETS + 4,)), dma((SETS, 3)), dma((SETS, 2, nz)), dma((SETS, 2, nz)),
                dma((3, PIECES)), dma((5,)), dma((2, REACH)), dma((2, 3)),
            ],
            compiler_params=pltpu.CompilerParams(
                collective_id=0, has_side_effects=True, vmem_limit_bytes=60 * 2**20),
        )(tokens, norm_gain[None, :], *halves, ids)

    in_specs = (
        P(("groups", "seq"), None),
        P(),
        P("seq", None),
        P("seq", None),
        P("seq", None),
        P(("groups", "seq")),
    )
    out_specs = P(("groups", "seq"), None)
    return jax.shard_map(on_device, mesh=mesh, in_specs=in_specs, out_specs=out_specs, check_vma=False)
```
